128 devices in a mesh: dp: 16 (over y, z_lo, core), mp: 8 (over z_hi, x).
Axes of the slice: x: 4, y: 4, z: 4 (z_hi: 2, z_lo: 2; z = z_hi * 2 + z_lo), core: 2. Of those that a mesh axis runs over, the one named last changes fastest.
Arguments:
- doc_ids: int32 [16, 512], P('dp'), may hold values from 0 to 128255
- doc_lengths: int32 [16], P('dp'), may hold values from 128 to 512
- activations: bfloat16 [8192, 4096], P('dp'), may hold values from -6 to 6
- out_grads: bfloat16 [8192, 14336], P('dp'), may hold values from -0.29882812 to 0.29882812
- input_basis: bfloat16 [4096, 2048], P(None, 'mp'), may hold values from -0.09375 to 0.09375
- output_basis: bfloat16 [14336, 7168], P('dp', 'mp'), may hold values from -0.046875 to 0.046875
- eigenvalues: bfloat16 [2048, 7168], P(None, 'mp'), may hold values from 0.5 to 50
- query_left: bfloat16 [64, 32, 2048], P('dp'), may hold values from -0.125 to 0.125
- query_right: bfloat16 [64, 32, 7168], P('dp', None, 'mp'), may hold values from -0.0625 to 0.0625
Outputs:
- scores: float32 [16, 64], P('dp')
The draws below stay inside these ranges and needn't reach their ends.
Inputs may be any that keep to these rules, and one draw needn't show every extreme that they name: `doc_lengths`: the live tokens are the first ones of each document.
All inputs are finite; a program needn't handle non-finite values.
Results may differ from the reference program's by a relative error of at most 0.023.
Values may be sent and summed in bfloat16 or wider, within the bound.
No kernel may reach another device: no remote copies, remote signals or barrier semaphores. Data moves between devices by JAX's collectives and lax.ppermute only.
A program may use at most 192 MiB of HBM per device.

```python
import math
import jax
import jax.numpy as jnp
import numpy as np
from jax import lax

D = 4096
FF = 14336
VOCAB = 128256
KIN = 2048
KOUT = 7168
RANK = 32
DOC_LEN = 512
DOCS = 16
QUERIES = 64
TOKENS = 8192
N_DP = 16


def plant(drawn, stream_key, least, largest):
    dims = drawn.shape
    place = [jax.random.randint(jax.random.fold_in(stream_key, axis), (), 0, dims[axis]) for axis in range(len(dims))]
    drawn = drawn.at[tuple(place)].set(least)
    longest = dims.index(max(dims))
    place[longest] = (place[longest] + 1) % dims[longest]
    return drawn.at[tuple(place)].set(largest)


def levels(stream_key, dims, pieces, low, top_value):
    loudness = 1.0
    for axis_at, parts in pieces:
        draws = jax.random.uniform(jax.random.fold_in(jax.random.fold_in(stream_key, 6), axis_at), (parts,), jnp.float32, low / len(pieces), top_value / len(pieces))
        loudness = loudness * jnp.repeat(jnp.exp(draws), dims[axis_at] // parts).reshape((-1,) + (1,) * (len(dims) - 1 - axis_at))
    return loudness


def skewed_wide(stream_key, shape, number_of, skew):
    weights = [min(1 << octave, number_of + 1 - (1 << octave)) * (1 << 20) // math.isqrt((1 << octave) ** skew) + 1 for octave in range((number_of + 1).bit_length()) if 1 << octave <= number_of]
    scale = 1 + sum(weights) // (1 << 30)
    table = np.cumsum(np.array([max(1, weight // scale) for weight in weights]))
    pick = jax.random.randint(jax.random.fold_in(stream_key, 1), shape, 0, int(table[len(weights) - 1]))
    start = jnp.left_shift(1, jnp.searchsorted(jnp.asarray(table, jnp.int32), pick, side="right").astype(jnp.int32))
    grade = start - 1 + jax.random.randint(jax.random.fold_in(stream_key, 4), shape, 0, 1 << 30) % jnp.minimum(start, number_of + 1 - start)
    return jax.random.permutation(jax.random.fold_in(stream_key, 2), number_of)[grade].astype(jnp.int32)


def gaussian(own_key, extent, scale, reach, shards=(), held_as=jnp.bfloat16):
    result = jax.random.normal(own_key, extent, jnp.float32) * scale
    if len(shards) > 0:
        result = levels(own_key, extent, shards, -0.22, 0.18) * result
    return jnp.clip(result, min=-reach, max=reach).astype(held_as)


def setup_inputs(seed: int = 0) -> dict:
    key_of = jax.random.split(jax.random.key(seed), 10)
    doc_ids = plant(skewed_wide(key_of[0], (DOCS, DOC_LEN), VOCAB, 2), jax.random.fold_in(key_of[0], 3), 0, VOCAB - 1).astype(jnp.int32)
    doc_lengths = plant(jax.random.randint(key_of[1], (DOCS,), DOC_LEN // 4, DOC_LEN + 1), jax.random.fold_in(key_of[1], 1), DOC_LEN // 4, DOC_LEN).astype(jnp.int32)
    activations = gaussian(key_of[2], (TOKENS, D), 1.0, 6.0, ((0, 16),))
    out_grads = gaussian(key_of[3], (TOKENS, FF), 0.05, 0.29882812, ((0, 16),))
    input_basis = gaussian(key_of[4], (D, KIN), D ** -0.5, 0.09375, ((1, 8),))
    output_basis = gaussian(key_of[5], (FF, KOUT), FF ** -0.5, 0.046875, ((0, 16), (1, 8)))
    eigenvalues = jnp.clip(jnp.exp(math.log(50.0) - 4.6051702 * jax.random.uniform(key_of[6], (KIN, KOUT), jnp.float32) ** levels(key_of[6], (KIN, KOUT), ((1, 8),), -0.2, 0.2)), 0.5, 50.0).astype(jnp.bfloat16)
    query_left = gaussian(key_of[7], (QUERIES, RANK, KIN), KIN ** -0.5, 0.125, ((0, 16),))
    query_right = gaussian(key_of[8], (QUERIES, RANK, KOUT), KOUT ** -0.5, 0.0625, ((0, 16), (2, 8)))
    return {"doc_ids": doc_ids, "doc_lengths": doc_lengths, "activations": activations, "out_grads": out_grads, "input_basis": input_basis, "output_basis": output_basis, "eigenvalues": eigenvalues, "query_left": query_left, "query_right": query_right}


damping = 0.5


def token_weights(doc_ids, doc_lengths):
    positions = jnp.arange(doc_ids.shape[1], dtype=jnp.int32)
    active = positions[None, :] < doc_lengths[:, None]
    matches = (doc_ids[:, :, None] == doc_ids[:, None, :]) & active[:, None, :]
    repeats = jnp.sum(matches.astype(jnp.float32), axis=2)
    return jnp.where(active, 1.0 / jnp.maximum(repeats, 1.0), 0.0).astype(jnp.float32)


def reference(doc_ids, doc_lengths, activations, out_grads, input_basis, output_basis, eigenvalues, query_left, query_right):
    rotated_in = jnp.dot(activations, input_basis, preferred_element_type=jnp.float32).astype(jnp.bfloat16)
    width = FF // N_DP
    summed = jnp.zeros((TOKENS, KOUT), jnp.float32)
    for member in range(N_DP):
        partial_value = jnp.dot(out_grads[:, member * width:(member + 1) * width], output_basis[member * width:(member + 1) * width], preferred_element_type=jnp.float32)
        summed = summed + lax.optimization_barrier(partial_value.astype(jnp.bfloat16)).astype(jnp.float32)
    rotated_out = summed.astype(jnp.bfloat16)
    weights = token_weights(doc_ids, doc_lengths)
    left_rows = query_left.reshape(QUERIES * RANK, KIN)
    right_rows = query_right.reshape(QUERIES * RANK, KOUT).astype(jnp.float32)
    denominator = eigenvalues.astype(jnp.float32) + damping

    def per_document(doc_index):
        first = doc_index * DOC_LEN
        acts_doc = lax.dynamic_slice_in_dim(rotated_in, first, DOC_LEN, 0)
        grads_doc = lax.dynamic_slice_in_dim(rotated_out, first, DOC_LEN, 0)
        weight_doc = lax.dynamic_index_in_dim(weights, doc_index, 0, keepdims=False)
        scaled = (weight_doc[:, None] * grads_doc.astype(jnp.float32)).astype(jnp.bfloat16)
        gradient = jnp.dot(acts_doc.T, scaled, preferred_element_type=jnp.float32)
        conditioned = (gradient / denominator).astype(jnp.bfloat16)
        mixture = jnp.dot(left_rows, conditioned, preferred_element_type=jnp.float32)
        return jnp.sum((mixture * right_rows).reshape(QUERIES, RANK * KOUT), axis=1)

    return lax.map(per_document, jnp.arange(DOCS, dtype=jnp.int32))
```

```python
import jax
import jax.numpy as jnp
from jax import lax
from jax.experimental import pallas as pl
from jax.experimental.pallas import tpu as pltpu
from jax.sharding import Mesh, PartitionSpec as P

damping = 0.5
f32 = jnp.float32
bf16 = jnp.bfloat16


def shifted(value, axis, step):
    size = lax.axis_size(axis)
    return lax.ppermute(value, axis, [(i, (i + step) % size) for i in range(size)])


def token_weights(doc_ids, doc_lengths):
    positions = jnp.arange(doc_ids.shape[1], dtype=jnp.int32)
    active = positions[None, :] < doc_lengths[:, None]
    matches = (doc_ids[:, :, None] == doc_ids[:, None, :]) & active[:, None, :]
    repeats = jnp.sum(matches.astype(f32), axis=2)
    return jnp.where(active, 1.0 / jnp.maximum(repeats, 1.0), 0.0)


def score_kernel(
    core_ref, own_ref, peer_ref, weight_ref, acts_ref, eig_ref, left_a, left_b, right_a, right_b,
    out_ref, scaled_ref, cond_ref, sums_ref, *, steps_in, steps_half, rank, x_size,
):
    step = pl.program_id(0)
    rows_in = acts_ref.shape[0]
    rows_q = left_a.shape[0]

    @pl.when(step == 0)
    def _():
        total = own_ref[...] + peer_ref[...].astype(f32)
        rotated = total.astype(bf16).astype(f32)
        scaled_ref[...] = (weight_ref[...] * rotated).astype(bf16)

    @pl.when(step < steps_in)
    def _():
        gradient = jnp.dot(acts_ref[...], scaled_ref[...], preferred_element_type=f32)
        conditioned = gradient / (eig_ref[...].astype(f32) + damping)
        start = pl.multiple_of(jnp.minimum(step, steps_in - 1) * rows_in, rows_in)
        cond_ref[pl.ds(start, rows_in), :] = conditioned.astype(bf16)

    def scored(left, right, slot):
        mixture = jnp.dot(left[...], cond_ref[...], preferred_element_type=f32)
        product = mixture * right[...].astype(f32)
        groups = product.reshape(rows_q // rank, rank, product.shape[1])
        part = jnp.sum(groups, axis=1)
        start = pl.multiple_of(slot * (rows_q // rank), rows_q // rank)
        sums_ref[pl.ds(start, rows_q // rank), :] = part

    @pl.when((step >= steps_in) & (step < steps_in + steps_half))
    def _():
        scored(left_a, right_a, jnp.clip(step - steps_in, 0, steps_half - 1))

    @pl.when(step >= steps_in + steps_half)
    def _():
        scored(left_b, right_b, jnp.clip(step - steps_in, steps_half, 2 * steps_half - 1))

    @pl.when(step == steps_in + 2 * steps_half - 1)
    def _():
        number = sums_ref.shape[0]
        values = jnp.sum(sums_ref[...], axis=1, keepdims=True)
        source = lax.broadcasted_iota(jnp.int32, (number, number), 0)
        target = lax.broadcasted_iota(jnp.int32, (number, number), 1)
        half = number // 2
        chips = half // x_size
        which = source // half
        parity = jnp.where(which == 0, core_ref[0], 1 - core_ref[0])
        inner = source % half
        place = (2 * (inner % chips) + parity) * x_size + inner // chips
        picked = jnp.where(place == target, values, 0.0)
        out_ref[...] = jnp.sum(picked, axis=0, keepdims=True)


def scores_of(core, own, peer, weights, acts, eig, left_a, left_b, right_a, right_b, rank, x_size):
    kin, tokens = acts.shape
    cols = own.shape[1]
    half = left_a.shape[0]
    steps_in = 4
    steps_half = 2
    rows_in = kin // steps_in
    rows_q = half // steps_half
    number = 2 * half // rank

    def first(g, core):
        return (jnp.minimum(g, steps_in - 1), 0)

    def second(g, core):
        return (jnp.clip(g - steps_in, 0, steps_half - 1), 0)

    def third(g, core):
        return (jnp.clip(g - steps_in - steps_half, 0, steps_half - 1), 0)

    def whole(g, core):
        return (0, 0)

    import functools

    body = functools.partial(
        score_kernel, steps_in=steps_in, steps_half=steps_half, rank=rank, x_size=x_size
    )
    return pl.pallas_call(
        body,
        grid_spec=pltpu.PrefetchScalarGridSpec(
            num_scalar_prefetch=1,
            grid=(steps_in + 2 * steps_half,),
            in_specs=[
                pl.BlockSpec((tokens, cols), whole),
                pl.BlockSpec((tokens, cols), whole),
                pl.BlockSpec((tokens, 1), whole),
                pl.BlockSpec((rows_in, tokens), first),
                pl.BlockSpec((rows_in, cols), first),
                pl.BlockSpec((rows_q, kin), second),
                pl.BlockSpec((rows_q, kin), third),
                pl.BlockSpec((rows_q, cols), second),
                pl.BlockSpec((rows_q, cols), third),
            ],
            out_specs=pl.BlockSpec((1, number), whole),
            scratch_shapes=[
                pltpu.VMEM((tokens, cols), bf16),
                pltpu.VMEM((kin, cols), bf16),
                pltpu.VMEM((number, cols), f32),
            ],
        ),
        out_shape=jax.ShapeDtypeStruct((1, number), f32),
        compiler_params=pltpu.CompilerParams(
            dimension_semantics=("arbitrary",), vmem_limit_bytes=48 * 1024 * 1024
        ),
        name="scores",
    )(core, own, peer, weights, acts, eig, left_a, left_b, right_a, right_b)


def per_device(
    doc_ids,
    doc_lengths,
    activations,
    out_grads,
    input_basis,
    output_basis,
    eigenvalues,
    query_left,
    query_right,
):
    tokens = activations.shape[0]
    rows, cols = output_basis.shape
    queries, rank, kin = query_left.shape
    n_y, n_zl, n_c = lax.axis_size("y"), lax.axis_size("zl"), lax.axis_size("c")
    n_zh, n_x = lax.axis_size("zh"), lax.axis_size("x")
    y, zl, core = lax.axis_index("y"), lax.axis_index("zl"), lax.axis_index("c")
    zh, x = lax.axis_index("zh"), lax.axis_index("x")
    chips = n_y * n_zl
    tile = 128

    block = jnp.concatenate([output_basis, query_right.reshape(queries * rank, cols)], axis=0)
    forth = lambda v: shifted(v, "y", 1)
    back = lambda v: shifted(v, "y", -1)
    across = lambda v: shifted(v, "zl", 1)
    sibling = lambda v: shifted(v, "c", 1)

    before, after, beside = forth(block), back(block), across(block)
    grads_out = jnp.stack(
        [
            lax.dynamic_slice(out_grads, (0, (2 * k + 1 - core) * rows), (tokens, rows))
            for k in range(chips)
        ]
    )
    grads_peer = sibling(grads_out)

    cut = 4 * tile
    before_beside_a = forth(beside[:cut])
    after_beside_a = back(beside[:cut])
    before_beside_b = across(before[cut:])
    after_beside_b = across(after[cut:])
    far_a = forth(before[:cut])
    far_b = back(after[cut:])
    far_beside_a = forth(before_beside_a[: 3 * tile])
    far_beside_b = across(far_a[3 * tile :])
    far_beside_c = back(after_beside_b[: 3 * tile])
    far_beside_d = across(far_b[3 * tile :])

    def chip(dy, dz):
        return ((y + dy) % n_y) * n_zl + (zl + dz) % n_zl

    pieces = [
        (chip(0, 0), 0, output_basis),
        (chip(3, 0), 0, before[:rows]),
        (chip(1, 0), 0, after[:rows]),
        (chip(0, 1), 0, beside[:rows]),
        (chip(3, 1), 0, before_beside_a),
        (chip(1, 1), 0, after_beside_a),
        (chip(3, 1), cut, before_beside_b[: rows - cut]),
        (chip(1, 1), cut, after_beside_b[: rows - cut]),
        (chip(2, 0), 0, far_a),
        (chip(2, 0), cut, far_b[: rows - cut]),
        (chip(2, 1), 0, far_beside_a),
        (chip(2, 1), 3 * tile, far_beside_b),
        (chip(2, 1), cut, far_beside_c),
    ]
    running_own = jnp.zeros((tokens, cols), f32)
    running_peer = jnp.zeros((tokens, cols), f32)
    for k, offset, piece in pieces:
        deep = piece.shape[0]
        mine = lax.dynamic_slice(out_grads, (0, (2 * k + core) * rows + offset), (tokens, deep))
        theirs = lax.dynamic_slice(grads_peer, (k, 0, offset), (1, tokens, deep))[0]
        running_peer = running_peer + jnp.dot(theirs, piece, preferred_element_type=f32)
        running_own = running_own + jnp.dot(mine, piece, preferred_element_type=f32)
    from_peer = sibling(running_peer.astype(bf16))

    share = lax.dot_general(
        input_basis, activations, (((0,), (1,)), ((), ())), preferred_element_type=f32
    ).astype(bf16)
    other = shifted(share, "zh", 1)
    pair = jnp.where(zh == 0, jnp.stack([share, other]), jnp.stack([other, share]))
    acts = lax.all_gather(pair, "x", axis=0)
    acts = jnp.swapaxes(acts, 0, 1).reshape(kin, tokens)

    mine_left = lax.dynamic_index_in_dim(query_left, x, 0, keepdims=False)
    left_chips = lax.all_to_all(
        jnp.broadcast_to(mine_left[None], (chips, rank, kin)), ("y", "zl"), 0, 0, tiled=True
    )
    left_own = lax.all_gather(left_chips, "x", axis=0).reshape(n_x * chips * rank, kin)
    left_peer = sibling(left_own)

    right_rows = queries * rank
    right_pieces = [
        (chip(0, 0), block[rows:]),
        (chip(3, 0), before[rows:]),
        (chip(1, 0), after[rows:]),
        (chip(0, 1), beside[rows:]),
        (chip(3, 1), before_beside_b[rows - cut :]),
        (chip(1, 1), after_beside_b[rows - cut :]),
        (chip(2, 0), far_b[rows - cut :]),
        (chip(2, 1), far_beside_d),
    ]
    right_own = jnp.zeros((n_x, chips, rank, cols), bf16)
    for k, piece in right_pieces:
        right_own = lax.dynamic_update_slice(
            right_own, piece.reshape(queries, 1, rank, cols), (0, k, 0, 0)
        )
    right_own = right_own.reshape(n_x * chips * rank, cols)
    right_peer = sibling(right_own)

    weights = token_weights(doc_ids, doc_lengths).reshape(tokens, 1)
    values = scores_of(
        core.reshape(1).astype(jnp.int32), running_own, from_peer, weights, acts, eigenvalues,
        left_own, left_peer, right_own, right_peer, rank, n_x,
    )
    values = values + lax.ppermute(values, "x", [(i, i ^ 1) for i in range(n_x)])
    values = values + lax.ppermute(values, "x", [(i, n_x - 1 - i) for i in range(n_x)])
    return values + shifted(values, "zh", 1)


def solution(mesh):
    parts = Mesh(mesh.devices.reshape(4, 2, 2, 2, 4), ("y", "zl", "c", "zh", "x"))
    dp, mp = ("y", "zl", "c"), ("zh", "x")
    return jax.shard_map(
        per_device,
        mesh=parts,
        in_specs=(
            P(dp, None),
            P(dp),
            P(dp, None),
            P(dp, None),
            P(None, mp),
            P(dp, mp),
            P(None, mp),
            P(dp, None, None),
            P(dp, None, mp),
        ),
        out_specs=P(dp, None),
        check_vma=False,
    )
```

```python
import functools

import jax
import jax.numpy as jnp
from jax import lax
from jax.experimental import pallas as pl
from jax.experimental.pallas import tpu as pltpu
from jax.sharding import Mesh, PartitionSpec as P

damping = 0.5
f32 = jnp.float32
bf16 = jnp.bfloat16


def shifted(value, axis, step):
    size = lax.axis_size(axis)
    return lax.ppermute(value, axis, [(i, (i + step) % size) for i in range(size)])


def token_weights(doc_ids, doc_lengths):
    positions = jnp.arange(doc_ids.shape[1], dtype=jnp.int32)
    active = positions[None, :] < doc_lengths[:, None]
    matches = (doc_ids[:, :, None] == doc_ids[:, None, :]) & active[:, None, :]
    repeats = jnp.sum(matches.astype(f32), axis=2)
    return jnp.where(active, 1.0 / jnp.maximum(repeats, 1.0), 0.0)


def score_kernel(
    chips_ref, tiles_ref, core_ref, mine, more, own_weight_ref, peer_weight_ref, own_acts,
    peer_acts, eig, left, *refs,
):
    rights = refs[:8]
    own_out, peer_out = refs[8:10]
    (
        mine_ref, more_ref, acts_ref, eig_ref, left_ref, right_ref, scaled_ref, cond_ref, sums_ref,
        sems, tile_sems,
    ) = refs[10:]
    tiles, rows_in, tokens = own_acts.shape
    n_x, chips, rank, kin = left.shape
    cols = eig.shape[1]
    tile = 128
    queries = n_x * chips

    tile_copies = []
    for at in range(tiles):
        start = pl.multiple_of(tiles_ref[at] * rows_in, rows_in)
        tile_copies.append(
            [
                pltpu.make_async_copy(own_acts.at[at], acts_ref.at[0, at], tile_sems.at[0, at]),
                pltpu.make_async_copy(peer_acts.at[at], acts_ref.at[1, at], tile_sems.at[1, at]),
                pltpu.make_async_copy(
                    eig.at[pl.ds(start, rows_in), :],
                    eig_ref.at[pl.ds(start, rows_in), :],
                    tile_sems.at[2, at],
                ),
            ]
        )
    left_copy = pltpu.make_async_copy(left, left_ref, sems.at[3])
    right_copies = [
        [
            pltpu.make_async_copy(
                piece.at[pl.ds(piece.shape[0] - tile + q * rank, rank), :],
                right_ref.at[q, chips_ref[index]],
                sems.at[4 + index * n_x + q],
            )
            for q in range(n_x)
        ]
        for index, piece in enumerate(rights)
    ]
    sum_copies = [
        pltpu.make_async_copy(mine, mine_ref, sems.at[4 + len(rights) * n_x]),
        pltpu.make_async_copy(more, more_ref, sems.at[5 + len(rights) * n_x]),
    ]
    for copy in sum_copies:
        copy.start()
    for group in tile_copies:
        for copy in group:
            copy.start()
    left_copy.start()
    for group in right_copies:
        for copy in group:
            copy.start()

    for copy in sum_copies:
        copy.wait()
    for index, (weight, mine_at, more_at) in enumerate(
        ((own_weight_ref, tokens, 0), (peer_weight_ref, 0, tokens))
    ):
        total = mine_ref[mine_at : mine_at + tokens, :].astype(f32)
        total = total + more_ref[more_at : more_at + tokens, :].astype(f32)
        rotated = total.astype(bf16).astype(f32)
        scaled_ref[index] = (weight[...] * rotated).astype(bf16)

    for first in range(0, tiles, 2):
        pair = (first, first + 1)
        for at in pair:
            for copy in tile_copies[at]:
                copy.wait()
        starts = [pl.multiple_of(tiles_ref[at] * rows_in, rows_in) for at in pair]
        scales = [
            1.0 / (eig_ref[pl.ds(start, rows_in), :].astype(f32) + damping) for start in starts
        ]
        for index in range(2):
            acts = acts_ref[index, first : first + 2].reshape(2 * rows_in, tokens)
            gradient = jnp.dot(acts, scaled_ref[index], preferred_element_type=f32)
            for half_at, (start, scale) in enumerate(zip(starts, scales)):
                cond_ref[pl.ds(start, rows_in), index * cols : (index + 1) * cols] = (
                    gradient[half_at * rows_in : (half_at + 1) * rows_in] * scale
                ).astype(bf16)

    left_copy.wait()
    for group in right_copies:
        for copy in group:
            copy.wait()
    wide = 2 * tile
    half = n_x // 2
    for part in range(2):
        rows = left_ref[part * half : (part + 1) * half].reshape(half * chips * rank, kin)
        for at in range(0, 2 * cols, wide):
            mixture = jnp.dot(rows, cond_ref[:, at : at + wide], preferred_element_type=f32)
            for one in range(at, at + wide, tile):
                index, column = one // cols, one % cols
                right = right_ref[part * half : (part + 1) * half, :, :, column : column + tile]
                right = right.reshape(half * chips * rank, tile).astype(f32)
                product = mixture[:, one - at : one - at + tile] * right
                groups = jnp.sum(product.reshape(half * chips, rank, tile), axis=1)
                rows_at = part * half * chips
                if column == 0:
                    sums_ref[index, rows_at : rows_at + half * chips, :] = groups
                else:
                    sums_ref[index, rows_at : rows_at + half * chips, :] += groups

    number = own_out.shape[1]
    source = lax.broadcasted_iota(jnp.int32, (queries, number), 0)
    target = lax.broadcasted_iota(jnp.int32, (queries, number), 1)
    place = (2 * (source % chips) + core_ref[0]) * n_x + source // chips
    for index, out in enumerate((own_out, peer_out)):
        values = jnp.sum(sums_ref[index], axis=1, keepdims=True)
        out[...] = jnp.sum(jnp.where(place == target, values, 0.0), axis=0, keepdims=True)


def scores_of(chips_at, tiles_at, core, mine, more, weights, acts, eig, left, rights, number):
    tokens = acts[0].shape[2]
    kin, cols = eig.shape
    n_x, chips, rank, _ = left.shape
    scalars = pl.BlockSpec(memory_space=pltpu.SMEM)
    held = pl.BlockSpec(memory_space=pltpu.VMEM)
    anywhere = pl.BlockSpec(memory_space=pltpu.HBM)
    return pl.pallas_call(
        score_kernel,
        in_specs=[*[scalars] * 3, *[anywhere] * 2, *[held] * 2, *[anywhere] * 12],
        out_specs=[held, held],
        scratch_shapes=[
            pltpu.VMEM(mine.shape, bf16),
            pltpu.VMEM(more.shape, bf16),
            pltpu.VMEM((2, *acts[0].shape), bf16),
            pltpu.VMEM(eig.shape, bf16),
            pltpu.VMEM(left.shape, bf16),
            pltpu.VMEM((n_x, chips, rank, cols), bf16),
            pltpu.VMEM((2, tokens, cols), bf16),
            pltpu.VMEM((kin, 2 * cols), bf16),
            pltpu.VMEM((2, n_x * chips, 128), f32),
            pltpu.SemaphoreType.DMA((6 + 8 * n_x,)),
            pltpu.SemaphoreType.DMA((3, acts[0].shape[0])),
        ],
        out_shape=[jax.ShapeDtypeStruct((1, number), f32)] * 2,
        compiler_params=pltpu.CompilerParams(vmem_limit_bytes=62 * 1024 * 1024),
        name="scores",
    )(chips_at, tiles_at, core, mine, more, *weights, *acts, eig, left, *rights)


def cut_kernel(*refs, cuts):
    count = len(cuts)
    sems = refs[-1]
    copies = [
        pltpu.make_async_copy(
            refs[at].at[pl.ds(start, size)], refs[count + at], sems.at[at]
        )
        for at, (start, size) in enumerate(cuts)
    ]
    for copy in copies:
        copy.start()
    for copy in copies:
        copy.wait()


def cut_out(arrays, cuts):
    return pl.pallas_call(
        functools.partial(cut_kernel, cuts=cuts),
        in_specs=[pl.BlockSpec(memory_space=pltpu.HBM)] * len(arrays),
        out_specs=[pl.BlockSpec(memory_space=pltpu.VMEM)] * len(arrays),
        out_shape=[
            jax.ShapeDtypeStruct((size, array.shape[1]), array.dtype)
            for array, (_, size) in zip(arrays, cuts)
        ],
        scratch_shapes=[pltpu.SemaphoreType.DMA((len(arrays),))],
        name="cut",
    )(*arrays)


def accumulate_kernel(places_ref, mine, theirs, *refs, plan, carried):
    count = sum(len(cuts) for cuts in plan)
    pieces = refs[:count]
    before = refs[count] if carried else None
    out_ref, grads_ref, basis_ref = refs[count + carried : count + carried + 3]
    sems = refs[-1]
    tokens = mine.shape[0]
    rows = sum(deep for _, deep in plan[0])

    groups = []
    used = 0
    at = 0
    for index, cuts in enumerate(plan):
        if index % 2 == 0:
            groups.append([])
        column = pl.multiple_of(places_ref[index] * rows, 128)
        for row, source in ((0, theirs), (tokens, mine)):
            groups[-1].append(
                pltpu.make_async_copy(
                    source.at[:, pl.ds(column, rows)],
                    grads_ref.at[pl.ds(row, tokens), pl.ds(index * rows, rows)],
                    sems.at[used],
                )
            )
            used += 1
        for offset, deep in cuts:
            groups[-1].append(
                pltpu.make_async_copy(
                    pieces[at].at[pl.ds(0, deep)],
                    basis_ref.at[pl.ds(index * rows + offset, deep)],
                    sems.at[used],
                )
            )
            used += 1
            at += 1
    for group in groups:
        for copy in group:
            copy.start()
    total = before[...] if carried else None
    for index, group in enumerate(groups):
        for copy in group:
            copy.wait()
        first, last = 2 * index * rows, min(2 * index + 2, len(plan)) * rows
        product = jnp.dot(
            grads_ref[:, first:last], basis_ref[first:last, :], preferred_element_type=f32
        )
        total = product if total is None else total + product
    out_ref[...] = total.astype(out_ref.dtype)


def accumulate(places, mine, theirs, plan, pieces, carried, kind):
    tokens = mine.shape[0]
    rows = sum(deep for _, deep in plan[0])
    cols = pieces[0].shape[1]
    held = pl.BlockSpec(memory_space=pltpu.VMEM)
    anywhere = pl.BlockSpec(memory_space=pltpu.HBM)
    return pl.pallas_call(
        functools.partial(accumulate_kernel, plan=plan, carried=len(carried)),
        in_specs=[
            pl.BlockSpec(memory_space=pltpu.SMEM),
            *[anywhere] * (2 + len(pieces)),
            *[held for _ in carried],
        ],
        out_specs=held,
        out_shape=jax.ShapeDtypeStruct((2 * tokens, cols), kind),
        scratch_shapes=[
            pltpu.VMEM((2 * tokens, len(plan) * rows), bf16),
            pltpu.VMEM((len(plan) * rows, cols), bf16),
            pltpu.SemaphoreType.DMA((2 * len(plan) + len(pieces),)),
        ],
        compiler_params=pltpu.CompilerParams(vmem_limit_bytes=62 * 1024 * 1024),
        name="accumulate",
    )(places, mine, theirs, *pieces, *carried)


def per_device(
    doc_ids,
    doc_lengths,
    activations,
    out_grads,
    input_basis,
    output_basis,
    eigenvalues,
    query_left,
    query_right,
):
    tokens = activations.shape[0]
    rows, cols = output_basis.shape
    queries, rank, kin = query_left.shape
    n_y, n_zl = lax.axis_size("y"), lax.axis_size("zl")
    n_x = lax.axis_size("x")
    y, zl, core = lax.axis_index("y"), lax.axis_index("zl"), lax.axis_index("c")
    zh, x = lax.axis_index("zh"), lax.axis_index("x")
    chips = n_y * n_zl
    tile = 128

    def forth(v):
        return shifted(v, "y", 1)

    def back(v):
        return shifted(v, "y", -1)

    def across(v):
        return shifted(v, "zl", 1)

    def sibling(v):
        return shifted(v, "c", 1)

    def chip(dy, dz):
        return ((y + dy) % n_y) * n_zl + (zl + dz) % n_zl

    def places(*relative):
        return jnp.stack([2 * chip(dy, dz) + core for dy, dz in relative]).astype(jnp.int32)

    def x_shift(v, step):
        return shifted(v, "x", step)

    mine_left = lax.dynamic_index_in_dim(query_left, x, 0, keepdims=False)
    left_dp = lax.all_gather(mine_left, ("y", "zl", "c"), axis=0)

    grads_peer = sibling(out_grads)
    share = lax.dot_general(
        input_basis, activations, (((0,), (1,)), ((), ())), preferred_element_type=f32
    ).astype(bf16)
    share, output_basis, query_right = lax.optimization_barrier(
        (share, output_basis, query_right)
    )
    other = shifted(share, "zh", 1)

    block = jnp.concatenate([output_basis, query_right.reshape(queries * rank, cols)], axis=0)
    before, after = forth(block), back(block)
    block_z, other = lax.optimization_barrier((block, other))
    beside = across(block_z)

    pair = jnp.where(zh == 0, jnp.stack([share, other]), jnp.stack([other, share]))
    weights = token_weights(doc_ids, doc_lengths)
    weights_peer = sibling(weights)
    pair, grads_peer, weights_peer = lax.optimization_barrier((pair, grads_peer, weights_peer))
    pair_before, pair_after = x_shift(pair, 1), x_shift(pair, -1)
    left_dp, pair_before, pair_after = lax.optimization_barrier((left_dp, pair_before, pair_after))
    left_chips = lax.dynamic_index_in_dim(
        left_dp.reshape(chips, 2, rank, kin), core, 1, keepdims=False
    )
    pair_far_0 = x_shift(pair_before[:1], 1)
    pair_far_1 = x_shift(pair_after[1:], -1)
    n_zh = lax.axis_size("zh")
    tiles_at = jnp.stack(
        [h * n_x + (x + dx) % n_x for dx in (0, -1, 1) for h in range(n_zh)]
        + [h * n_x + (x + 2) % n_x for h in range(n_zh)]
    ).astype(jnp.int32)
    chips_at = jnp.stack(
        [
            chip(0, 0), chip(3, 0), chip(1, 0), chip(0, 1),
            chip(3, 1), chip(1, 1), chip(2, 0), chip(2, 1),
        ]
    ).astype(jnp.int32)
    core_at = core.reshape(1).astype(jnp.int32)
    places_a = places((0, 0), (3, 0), (1, 0), (0, 1))
    places_b = places((2, 0), (3, 1), (1, 1))
    places_c = places((2, 1))
    weights = weights.reshape(tokens, 1)
    weights_peer = weights_peer.reshape(tokens, 1)
    (
        before, after, beside, weights, weights_peer, left_chips, pair_far_0, pair_far_1, tiles_at,
        chips_at, core_at, places_a, places_b, places_c,
    ) = lax.optimization_barrier(
        (
            before, after, beside, weights, weights_peer, left_chips, pair_far_0, pair_far_1,
            tiles_at, chips_at, core_at, places_a, places_b, places_c,
        )
    )

    left = lax.all_gather(left_chips, "x", axis=0)
    far = forth(before)
    after_beside = back(beside)
    before_beside = across(before)
    one = ((0, rows),)
    sums = accumulate(
        places_a, out_grads, grads_peer, (one, one, one, one),
        (output_basis, before, after, beside), (), f32,
    )
    sums, pair, pair_before, pair_after, pair_far_0, pair_far_1 = lax.optimization_barrier(
        (sums, pair, pair_before, pair_after, pair_far_0, pair_far_1)
    )
    acts = jnp.concatenate([pair, pair_before, pair_after, pair_far_0, pair_far_1])
    far, after_beside, before_beside, sums, acts = lax.optimization_barrier(
        (far, after_beside, before_beside, sums, acts)
    )
    acts_peer = sibling(acts)

    part_a, part_b, part_c = cut_out(
        (before_beside, after_beside, far),
        ((0, 3 * tile), (3 * tile, 3 * tile), (6 * tile, far.shape[0] - 6 * tile)),
    )
    far_beside_a, far_beside_b, far_beside_c = forth(part_a), back(part_b), across(part_c)
    sums = accumulate(
        places_b, out_grads, grads_peer, (one, one, one),
        (far, before_beside, after_beside), (sums,), f32,
    )
    three = ((0, 3 * tile), (3 * tile, 3 * tile), (6 * tile, tile))
    mine = accumulate(
        places_c, out_grads, grads_peer, (three,),
        (far_beside_a, far_beside_b, far_beside_c), (sums,), bf16,
    )
    more = sibling(mine)

    rights = (
        block, before, after, beside, before_beside, after_beside, far, far_beside_c,
    )
    values, values_peer = scores_of(
        chips_at, tiles_at, core_at, mine, more,
        (weights, weights_peer), (acts, acts_peer),
        eigenvalues, left, rights, queries * 2 * chips,
    )
    values = values + sibling(values_peer)
    values = values + lax.ppermute(values, "x", [(i, i ^ 1) for i in range(n_x)])
    values = values + lax.ppermute(values, "x", [(i, n_x - 1 - i) for i in range(n_x)])
    return values + shifted(values, "zh", 1)


def solution(mesh):
    parts = Mesh(mesh.devices.reshape(4, 2, 2, 2, 4), ("y", "zl", "c", "zh", "x"))
    dp, mp = ("y", "zl", "c"), ("zh", "x")
    return jax.shard_map(
        per_device,
        mesh=parts,
        in_specs=(
            P(dp, None),
            P(dp),
            P(dp, None),
            P(dp, None),
            P(None, mp),
            P(dp, mp),
            P(None, mp),
            P(dp, None, None),
            P(dp, None, mp),
        ),
        out_specs=P(dp, None),
        check_vma=False,
    )
```

```python
import functools

import jax
import jax.numpy as jnp
from jax import lax
from jax.experimental import pallas as pl
from jax.experimental.pallas import tpu as pltpu
from jax.sharding import Mesh, PartitionSpec as P

damping = 0.5
f32 = jnp.float32
bf16 = jnp.bfloat16


def shifted(value, axis, step):
    size = lax.axis_size(axis)
    return lax.ppermute(value, axis, [(i, (i + step) % size) for i in range(size)])


def token_weights(doc_ids, doc_lengths):
    positions = jnp.arange(doc_ids.shape[1], dtype=jnp.int32)
    active = positions[None, :] < doc_lengths[:, None]
    matches = (doc_ids[:, :, None] == doc_ids[:, None, :]) & active[:, None, :]
    repeats = jnp.sum(matches.astype(f32), axis=2)
    return jnp.where(active, 1.0 / jnp.maximum(repeats, 1.0), 0.0)


def score_kernel(
    chips_ref, tiles_ref, core_ref, mine, more, own_weight, peer_weight, own_acts,
    peer_acts, eig, left, *refs, right_rows, count,
):
    rights = refs[:count]
    own_out, peer_out = refs[count : count + 2]
    (
        mine_ref, more_ref, acts_ref, eig_ref, left_ref, right_ref, scaled_ref, cond_ref, sums_ref,
        sems, tile_sems, weights_ref,
    ) = refs[count + 2 :]
    tiles, rows_in, tokens = own_acts.shape
    n_x, chips, rank, kin = left.shape
    cols = eig.shape[1]
    tile = 128
    queries = n_x * chips

    tile_copies = []
    for at in range(tiles):
        start = pl.multiple_of(tiles_ref[at] * rows_in, rows_in)
        tile_copies.append(
            [
                pltpu.make_async_copy(own_acts.at[at], acts_ref.at[0, at], tile_sems.at[0, at]),
                pltpu.make_async_copy(peer_acts.at[at], acts_ref.at[1, at], tile_sems.at[1, at]),
                pltpu.make_async_copy(
                    eig.at[pl.ds(start, rows_in), :],
                    eig_ref.at[pl.ds(start, rows_in), :],
                    tile_sems.at[2, at],
                ),
            ]
        )
    left_copy = pltpu.make_async_copy(left, left_ref, sems.at[3])
    right_copies = [
        [
            pltpu.make_async_copy(
                rights[piece].at[pl.ds(row + q * rank, rank), :],
                right_ref.at[q, chips_ref[index]],
                sems.at[4 + index * n_x + q],
            )
            for q in range(n_x)
        ]
        for index, (piece, row) in enumerate(right_rows)
    ]
    sum_copies = [
        pltpu.make_async_copy(mine, mine_ref, sems.at[4 + len(right_rows) * n_x]),
        pltpu.make_async_copy(more, more_ref, sems.at[5 + len(right_rows) * n_x]),
        pltpu.make_async_copy(own_weight, weights_ref.at[0], sems.at[0]),
        pltpu.make_async_copy(peer_weight, weights_ref.at[1], sems.at[1]),
    ]
    for copy in sum_copies:
        copy.start()
    for group in tile_copies:
        for copy in group:
            copy.start()
    left_copy.start()
    for group in right_copies:
        for copy in group:
            copy.start()

    for copy in sum_copies:
        copy.wait()
    for index, (mine_at, more_at) in enumerate(((tokens, 0), (0, tokens))):
        total = mine_ref[mine_at : mine_at + tokens, :].astype(f32)
        total = total + more_ref[more_at : more_at + tokens, :].astype(f32)
        rotated = total.astype(bf16).astype(f32)
        scaled_ref[index] = (weights_ref[index] * rotated).astype(bf16)

    for first in range(0, tiles, 2):
        pair = (first, first + 1)
        for at in pair:
            for copy in tile_copies[at]:
                copy.wait()
        starts = [pl.multiple_of(tiles_ref[at] * rows_in, rows_in) for at in pair]
        scales = [
            1.0 / (eig_ref[pl.ds(start, rows_in), :].astype(f32) + damping) for start in starts
        ]
        for index in range(2):
            acts = acts_ref[index, first : first + 2].reshape(2 * rows_in, tokens)
            gradient = jnp.dot(acts, scaled_ref[index], preferred_element_type=f32)
            for half_at, (start, scale) in enumerate(zip(starts, scales)):
                cond_ref[pl.ds(start, rows_in), index * cols : (index + 1) * cols] = (
                    gradient[half_at * rows_in : (half_at + 1) * rows_in] * scale
                ).astype(bf16)

    left_copy.wait()
    for group in right_copies:
        for copy in group:
            copy.wait()
    wide = 2 * tile
    half = n_x // 2
    for part in range(2):
        rows = left_ref[part * half : (part + 1) * half].reshape(half * chips * rank, kin)
        for at in range(0, 2 * cols, wide):
            mixture = jnp.dot(rows, cond_ref[:, at : at + wide], preferred_element_type=f32)
            for one in range(at, at + wide, tile):
                index, column = one // cols, one % cols
                right = right_ref[part * half : (part + 1) * half, :, :, column : column + tile]
                right = right.reshape(half * chips * rank, tile).astype(f32)
                product = mixture[:, one - at : one - at + tile] * right
                groups = jnp.sum(product.reshape(half * chips, rank, tile), axis=1)
                rows_at = part * half * chips
                if column == 0:
                    sums_ref[index, rows_at : rows_at + half * chips, :] = groups
                else:
                    sums_ref[index, rows_at : rows_at + half * chips, :] += groups

    number = own_out.shape[1]
    source = lax.broadcasted_iota(jnp.int32, (queries, number), 0)
    target = lax.broadcasted_iota(jnp.int32, (queries, number), 1)
    place = (2 * (source % chips) + core_ref[0]) * n_x + source // chips
    for index, out in enumerate((own_out, peer_out)):
        values = jnp.sum(sums_ref[index], axis=1, keepdims=True)
        out[...] = jnp.sum(jnp.where(place == target, values, 0.0), axis=0, keepdims=True)


def scores_of(
    chips_at, tiles_at, core, mine, more, weights, acts, eig, left, rights, right_rows, number
):
    tokens = acts[0].shape[2]
    kin, cols = eig.shape
    n_x, chips, rank, _ = left.shape
    scalars = pl.BlockSpec(memory_space=pltpu.SMEM)
    held = pl.BlockSpec(memory_space=pltpu.VMEM)
    anywhere = pl.BlockSpec(memory_space=pltpu.HBM)
    return pl.pallas_call(
        functools.partial(score_kernel, right_rows=right_rows, count=len(rights)),
        in_specs=[*[scalars] * 3, *[anywhere] * (8 + len(rights))],
        out_specs=[held, held],
        scratch_shapes=[
            pltpu.VMEM(mine.shape, bf16),
            pltpu.VMEM(more.shape, bf16),
            pltpu.VMEM((2, *acts[0].shape), bf16),
            pltpu.VMEM(eig.shape, bf16),
            pltpu.VMEM(left.shape, bf16),
            pltpu.VMEM((n_x, chips, rank, cols), bf16),
            pltpu.VMEM((2, tokens, cols), bf16),
            pltpu.VMEM((kin, 2 * cols), bf16),
            pltpu.VMEM((2, n_x * chips, 128), f32),
            pltpu.SemaphoreType.DMA((6 + 8 * n_x,)),
            pltpu.SemaphoreType.DMA((3, acts[0].shape[0])),
            pltpu.VMEM((2, tokens, 1), f32),
        ],
        out_shape=[jax.ShapeDtypeStruct((1, number), f32)] * 2,
        compiler_params=pltpu.CompilerParams(vmem_limit_bytes=62 * 1024 * 1024),
        name="scores",
    )(chips_at, tiles_at, core, mine, more, *weights, *acts, eig, left, *rights)


def cut_kernel(*refs, cuts, count):
    sources, outs, sems = refs[:count], refs[count:-1], refs[-1]
    copies = [
        pltpu.make_async_copy(
            sources[source].at[pl.ds(start, size)], outs[out].at[pl.ds(to, size)], sems.at[at]
        )
        for at, (source, start, size, out, to) in enumerate(cuts)
    ]
    for copy in copies:
        copy.start()
    for copy in copies:
        copy.wait()


def cut_out(arrays, cuts):
    cols = arrays[0].shape[1]
    lengths = {}
    for _, _, size, out, to in cuts:
        lengths[out] = max(lengths.get(out, 0), to + size)
    return pl.pallas_call(
        functools.partial(cut_kernel, cuts=cuts, count=len(arrays)),
        in_specs=[pl.BlockSpec(memory_space=pltpu.HBM)] * len(arrays),
        out_specs=[pl.BlockSpec(memory_space=pltpu.VMEM)] * len(lengths),
        out_shape=[
            jax.ShapeDtypeStruct((lengths[out], cols), arrays[0].dtype)
            for out in range(len(lengths))
        ],
        scratch_shapes=[pltpu.SemaphoreType.DMA((len(cuts),))],
        name="cut",
    )(*arrays)


def accumulate_kernel(places_ref, mine, theirs, *refs, plan, count, carried):
    pieces = refs[:count]
    out_ref, grads_ref, basis_ref, sems = refs[count + carried : count + carried + 4]
    tokens = mine.shape[0]
    rows = sum(deep for _, deep, _, _ in plan[0])
    bounds = list(range(len(plan), 0, -2))[::-1]
    starts = [0] + bounds[:-1]

    groups = []
    used = 0
    for first, last in zip(starts, bounds):
        group = []
        for index in range(first, last):
            column = pl.multiple_of(places_ref[index] * rows, 128)
            for row, source in ((0, theirs), (tokens, mine)):
                group.append(
                    pltpu.make_async_copy(
                        source.at[:, pl.ds(column, rows)],
                        grads_ref.at[pl.ds(row, tokens), pl.ds(index * rows, rows)],
                        sems.at[used],
                    )
                )
                used += 1
            for offset, deep, piece, piece_row in plan[index]:
                group.append(
                    pltpu.make_async_copy(
                        pieces[piece].at[pl.ds(piece_row, deep)],
                        basis_ref.at[pl.ds(index * rows + offset, deep)],
                        sems.at[used],
                    )
                )
                used += 1
        groups.append(group)
    for group in groups:
        for copy in group:
            copy.start()
    if carried:
        before_ref = refs[-1]
        carry = pltpu.make_async_copy(refs[count], before_ref, sems.at[used])
        carry.start()
    total = None
    for first, last, group in zip(starts, bounds, groups):
        for copy in group:
            copy.wait()
        product = jnp.dot(
            grads_ref[:, first * rows : last * rows],
            basis_ref[first * rows : last * rows, :],
            preferred_element_type=f32,
        )
        total = product if total is None else total + product
    if carried:
        carry.wait()
        total = total + before_ref[...]
    out_ref[...] = total.astype(out_ref.dtype)


def accumulate(places, mine, theirs, plan, pieces, carried, kind):
    tokens = mine.shape[0]
    rows = sum(deep for _, deep, _, _ in plan[0])
    cols = pieces[0].shape[1]
    held = pl.BlockSpec(memory_space=pltpu.VMEM)
    anywhere = pl.BlockSpec(memory_space=pltpu.HBM)
    copies = sum(2 + len(cuts) for cuts in plan) + 1
    return pl.pallas_call(
        functools.partial(
            accumulate_kernel, plan=plan, count=len(pieces), carried=len(carried)
        ),
        in_specs=[
            pl.BlockSpec(memory_space=pltpu.SMEM),
            *[anywhere] * (2 + len(pieces) + len(carried)),
        ],
        out_specs=held,
        out_shape=jax.ShapeDtypeStruct((2 * tokens, cols), kind),
        scratch_shapes=[
            pltpu.VMEM((2 * tokens, len(plan) * rows), bf16),
            pltpu.VMEM((len(plan) * rows, cols), bf16),
            pltpu.SemaphoreType.DMA((copies,)),
            *[pltpu.VMEM((2 * tokens, cols), f32) for _ in carried],
        ],
        compiler_params=pltpu.CompilerParams(vmem_limit_bytes=62 * 1024 * 1024),
        name="accumulate",
    )(places, mine, theirs, *pieces, *carried)


def per_device(
    doc_ids,
    doc_lengths,
    activations,
    out_grads,
    input_basis,
    output_basis,
    eigenvalues,
    query_left,
    query_right,
):
    tokens = activations.shape[0]
    rows, cols = output_basis.shape
    queries, rank, kin = query_left.shape
    n_y, n_zl = lax.axis_size("y"), lax.axis_size("zl")
    n_x = lax.axis_size("x")
    y, zl, core = lax.axis_index("y"), lax.axis_index("zl"), lax.axis_index("c")
    zh, x = lax.axis_index("zh"), lax.axis_index("x")
    chips = n_y * n_zl
    tile = 128

    def forth(v):
        return shifted(v, "y", 1)

    def back(v):
        return shifted(v, "y", -1)

    def across(v):
        return shifted(v, "zl", 1)

    def sibling(v):
        return shifted(v, "c", 1)

    def chip(dy, dz):
        return ((y + dy) % n_y) * n_zl + (zl + dz) % n_zl

    def places(*relative):
        return jnp.stack([2 * chip(dy, dz) + core for dy, dz in relative]).astype(jnp.int32)

    def x_shift(v, step):
        return shifted(v, "x", step)

    mine_left = lax.dynamic_index_in_dim(query_left, x, 0, keepdims=False)
    other_left = across(mine_left)
    left_pair = jnp.where(
        zl == 0, jnp.stack([mine_left, other_left]), jnp.stack([other_left, mine_left])
    )
    left_dp = lax.all_gather(left_pair, "y", axis=0)

    grads_peer = sibling(out_grads)
    share = lax.dot_general(
        input_basis, activations, (((0,), (1,)), ((), ())), preferred_element_type=f32
    ).astype(bf16)
    other = shifted(share, "zh", 1)

    block = jnp.concatenate([output_basis, query_right.reshape(queries * rank, cols)], axis=0)
    before, after = forth(block), back(block)
    half, most = 4 * tile, 5 * tile
    basis_z, right_z, other, left_pair = lax.optimization_barrier(
        (output_basis, query_right, other, left_pair)
    )
    beside_head = across(basis_z[:most])
    beside_end = across(
        jnp.concatenate([basis_z[most:], right_z.reshape(queries * rank, cols)], axis=0)
    )

    pair = jnp.where(zh == 0, jnp.stack([share, other]), jnp.stack([other, share]))
    weights = token_weights(doc_ids, doc_lengths)
    weights_peer = sibling(weights)
    pair, grads_peer, weights_peer = lax.optimization_barrier((pair, grads_peer, weights_peer))
    pair_before, pair_after = x_shift(pair, 1), x_shift(pair, -1)
    left_dp, pair_before, pair_after = lax.optimization_barrier((left_dp, pair_before, pair_after))
    left_chips = left_dp.reshape(chips, rank, kin)
    pair_far_0 = x_shift(pair_before[:1], 1)
    pair_far_1 = x_shift(pair_after[1:], -1)
    n_zh = lax.axis_size("zh")
    tiles_at = jnp.stack(
        [h * n_x + (x + dx) % n_x for dx in (0, -1, 1) for h in range(n_zh)]
        + [h * n_x + (x + 2) % n_x for h in range(n_zh)]
    ).astype(jnp.int32)
    chips_at = jnp.stack(
        [
            chip(0, 0), chip(3, 0), chip(1, 0), chip(0, 1),
            chip(3, 1), chip(1, 1), chip(2, 0), chip(2, 1),
        ]
    ).astype(jnp.int32)
    core_at = core.reshape(1).astype(jnp.int32)
    places_a = places((0, 0), (3, 0), (1, 0), (0, 1))
    places_c = places((2, 0), (3, 1), (1, 1))
    places_d = places((2, 1))
    weights = weights.reshape(tokens, 1)
    weights_peer = weights_peer.reshape(tokens, 1)
    (
        before, after, beside_head, weights, weights_peer, left_chips, pair_far_0, pair_far_1,
        tiles_at, chips_at, core_at, places_a, places_c, places_d,
    ) = lax.optimization_barrier(
        (
            before, after, beside_head, weights, weights_peer, left_chips, pair_far_0,
            pair_far_1, tiles_at, chips_at, core_at, places_a, places_c, places_d,
        )
    )

    left = lax.all_gather(left_chips, "x", axis=0)
    length = before.shape[0]
    end = length - most
    before_head, after_tail, both_ends = cut_out(
        (before, after),
        (
            (0, 0, half, 0, 0),
            (1, half, length - half, 1, 0),
            (0, most, end, 2, 0),
            (1, most, end, 2, end),
        ),
    )
    far_a, far_b = forth(before_head), back(after_tail)
    beside_ends = across(both_ends)
    before_beside_a, after_beside_a = forth(beside_head), back(beside_head)
    acts = jnp.concatenate([pair, pair_before, pair_after, pair_far_0, pair_far_1])
    before_beside_a, after_beside_a = forth(beside_head), back(beside_head)
    acts = jnp.concatenate([pair, pair_before, pair_after, pair_far_0, pair_far_1])
    sums = accumulate(
        places_a, out_grads, grads_peer,
        (
            ((0, rows, 0, 0),),
            ((0, rows, 1, 0),),
            ((0, rows, 2, 0),),
            ((0, most, 3, 0), (most, rows - most, 4, 0)),
        ),
        (output_basis, before, after, beside_head, beside_end), (), f32,
    )
    before_beside_a, after_beside_a, sums, acts = lax.optimization_barrier(
        (before_beside_a, after_beside_a, sums, acts)
    )

    part_a, part_b, part_c = cut_out(
        (before_beside_a, after_beside_a, far_b),
        (
            (0, 0, 3 * tile, 0, 0),
            (1, 3 * tile, 2 * tile, 1, 0),
            (2, most - half, end, 2, 0),
        ),
    )
    far_beside_a, far_beside_b, far_beside_c = forth(part_a), back(part_b), across(part_c)
    acts_peer = sibling(acts)
    sums = accumulate(
        places_c, out_grads, grads_peer,
        (
            ((0, half, 0, 0), (half, rows - half, 1, 0)),
            ((0, most, 2, 0), (most, rows - most, 4, 0)),
            ((0, most, 3, 0), (most, rows - most, 4, end)),
        ),
        (far_a, far_b, before_beside_a, after_beside_a, beside_ends), (sums,), f32,
    )

    mine = accumulate(
        places_d, out_grads, grads_peer,
        (((0, 3 * tile, 0, 0), (3 * tile, 2 * tile, 1, 0), (most, rows - most, 2, 0)),),
        (far_beside_a, far_beside_b, far_beside_c), (sums,), bf16,
    )
    more = sibling(mine)

    rights = (block, before, after, beside_end, beside_ends, far_b, far_beside_c)
    right_rows = (
        (0, rows), (1, rows), (2, rows), (3, end - tile), (4, end - tile), (4, 2 * end - tile),
        (5, far_b.shape[0] - tile), (6, end - tile),
    )
    values, values_peer = scores_of(
        chips_at, tiles_at, core_at, mine, more,
        (weights, weights_peer), (acts, acts_peer),
        eigenvalues, left, rights, right_rows, queries * 2 * chips,
    )
    values = values + sibling(values_peer)
    values = values + lax.ppermute(values, "x", [(i, i ^ 1) for i in range(n_x)])
    values = values + lax.ppermute(values, "x", [(i, n_x - 1 - i) for i in range(n_x)])
    return values + shifted(values, "zh", 1)


def solution(mesh):
    parts = Mesh(mesh.devices.reshape(4, 2, 2, 2, 4), ("y", "zl", "c", "zh", "x"))
    dp, mp = ("y", "zl", "c"), ("zh", "x")
    return jax.shard_map(
        per_device,
        mesh=parts,
        in_specs=(
            P(dp, None),
            P(dp),
            P(dp, None),
            P(dp, None),
            P(None, mp),
            P(dp, mp),
            P(None, mp),
            P(dp, None, None),
            P(dp, None, mp),
        ),
        out_specs=P(dp, None),
        check_vma=False,
    )
```

```python
import functools

import jax
import jax.numpy as jnp
from jax import lax
from jax.experimental import pallas as pl
from jax.experimental.pallas import tpu as pltpu
from jax.sharding import Mesh, PartitionSpec as P

damping = 0.5
f32 = jnp.float32
bf16 = jnp.bfloat16


def shifted(value, axis, step):
    size = lax.axis_size(axis)
    return lax.ppermute(value, axis, [(i, (i + step) % size) for i in range(size)])


def token_weights(doc_ids, doc_lengths):
    positions = jnp.arange(doc_ids.shape[1], dtype=jnp.int32)
    active = positions[None, :] < doc_lengths[:, None]
    matches = (doc_ids[:, :, None] == doc_ids[:, None, :]) & active[:, None, :]
    repeats = jnp.sum(matches.astype(f32), axis=2)
    return jnp.where(active, 1.0 / jnp.maximum(repeats, 1.0), 0.0)


def score_kernel(
    chips_ref, tiles_ref, core_ref, mine, more, own_weight, peer_weight, own_acts,
    peer_acts, eig, left, *refs, right_rows, count,
):
    rights = refs[:count]
    own_out, peer_out = refs[count : count + 2]
    (
        mine_ref, more_ref, acts_ref, eig_ref, left_ref, right_ref, scaled_ref, cond_ref, sums_ref,
        sems, tile_sems, weights_ref,
    ) = refs[count + 2 :]
    tiles, rows_in, tokens = own_acts.shape
    n_x, chips, rank, kin = left.shape
    cols = eig.shape[1]
    tile = 128
    queries = n_x * chips

    tile_copies = []
    for at in range(tiles):
        start = pl.multiple_of(tiles_ref[at] * rows_in, rows_in)
        tile_copies.append(
            [
                pltpu.make_async_copy(own_acts.at[at], acts_ref.at[0, at], tile_sems.at[0, at]),
                pltpu.make_async_copy(peer_acts.at[at], acts_ref.at[1, at], tile_sems.at[1, at]),
                pltpu.make_async_copy(
                    eig.at[pl.ds(start, rows_in), :],
                    eig_ref.at[pl.ds(start, rows_in), :],
                    tile_sems.at[2, at],
                ),
            ]
        )
    left_copy = pltpu.make_async_copy(left, left_ref, sems.at[3])
    right_copies = [
        [
            pltpu.make_async_copy(
                rights[piece].at[pl.ds(row + q * rank, rank), :],
                right_ref.at[q, chips_ref[index]],
                sems.at[4 + index * n_x + q],
            )
            for q in range(n_x)
        ]
        for index, (piece, row) in enumerate(right_rows)
    ]
    sum_copies = [
        pltpu.make_async_copy(mine, mine_ref, sems.at[4 + len(right_rows) * n_x]),
        pltpu.make_async_copy(more, more_ref, sems.at[5 + len(right_rows) * n_x]),
        pltpu.make_async_copy(own_weight, weights_ref.at[0], sems.at[0]),
        pltpu.make_async_copy(peer_weight, weights_ref.at[1], sems.at[1]),
    ]
    for copy in sum_copies:
        copy.start()
    for group in tile_copies:
        for copy in group:
            copy.start()
    left_copy.start()
    for group in right_copies:
        for copy in group:
            copy.start()

    for copy in sum_copies:
        copy.wait()
    for index, (mine_at, more_at) in enumerate(((tokens, 0), (0, tokens))):
        total = mine_ref[mine_at : mine_at + tokens, :].astype(f32)
        total = total + more_ref[more_at : more_at + tokens, :].astype(f32)
        rotated = total.astype(bf16).astype(f32)
        scaled_ref[index] = (weights_ref[index] * rotated).astype(bf16)

    for first in range(0, tiles, 2):
        pair = (first, first + 1)
        for at in pair:
            for copy in tile_copies[at]:
                copy.wait()
        starts = [pl.multiple_of(tiles_ref[at] * rows_in, rows_in) for at in pair]
        scales = [
            1.0 / (eig_ref[pl.ds(start, rows_in), :].astype(f32) + damping) for start in starts
        ]
        for index in range(2):
            acts = acts_ref[index, first : first + 2].reshape(2 * rows_in, tokens)
            gradient = jnp.dot(acts, scaled_ref[index], preferred_element_type=f32)
            for half_at, (start, scale) in enumerate(zip(starts, scales)):
                cond_ref[pl.ds(start, rows_in), index * cols : (index + 1) * cols] = (
                    gradient[half_at * rows_in : (half_at + 1) * rows_in] * scale
                ).astype(bf16)

    left_copy.wait()
    for group in right_copies:
        for copy in group:
            copy.wait()
    wide = 2 * tile
    half = n_x // 2
    for part in range(2):
        rows = left_ref[part * half : (part + 1) * half].reshape(half * chips * rank, kin)
        for at in range(0, 2 * cols, wide):
            mixture = jnp.dot(rows, cond_ref[:, at : at + wide], preferred_element_type=f32)
            for one in range(at, at + wide, tile):
                index, column = one // cols, one % cols
                right = right_ref[part * half : (part + 1) * half, :, :, column : column + tile]
                right = right.reshape(half * chips * rank, tile).astype(f32)
                product = mixture[:, one - at : one - at + tile] * right
                groups = jnp.sum(product.reshape(half * chips, rank, tile), axis=1)
                rows_at = part * half * chips
                if column == 0:
                    sums_ref[index, rows_at : rows_at + half * chips, :] = groups
                else:
                    sums_ref[index, rows_at : rows_at + half * chips, :] += groups

    number = own_out.shape[1]
    source = lax.broadcasted_iota(jnp.int32, (queries, number), 0)
    target = lax.broadcasted_iota(jnp.int32, (queries, number), 1)
    place = (2 * (source % chips) + core_ref[0]) * n_x + source // chips
    for index, out in enumerate((own_out, peer_out)):
        values = jnp.sum(sums_ref[index], axis=1, keepdims=True)
        out[...] = jnp.sum(jnp.where(place == target, values, 0.0), axis=0, keepdims=True)


def scores_of(
    chips_at, tiles_at, core, mine, more, weights, acts, eig, left, rights, right_rows, number
):
    tokens = acts[0].shape[2]
    kin, cols = eig.shape
    n_x, chips, rank, _ = left.shape
    scalars = pl.BlockSpec(memory_space=pltpu.SMEM)
    held = pl.BlockSpec(memory_space=pltpu.VMEM)
    anywhere = pl.BlockSpec(memory_space=pltpu.HBM)
    return pl.pallas_call(
        functools.partial(score_kernel, right_rows=right_rows, count=len(rights)),
        in_specs=[*[scalars] * 3, anywhere, held, *[anywhere] * (6 + len(rights))],
        out_specs=[held, held],
        scratch_shapes=[
            pltpu.VMEM(mine.shape, bf16),
            pltpu.VMEM(more.shape, bf16),
            pltpu.VMEM((2, *acts[0].shape), bf16),
            pltpu.VMEM(eig.shape, bf16),
            pltpu.VMEM(left.shape, bf16),
            pltpu.VMEM((n_x, chips, rank, cols), bf16),
            pltpu.VMEM((2, tokens, cols), bf16),
            pltpu.VMEM((kin, 2 * cols), bf16),
            pltpu.VMEM((2, n_x * chips, 128), f32),
            pltpu.SemaphoreType.DMA((6 + 8 * n_x,)),
            pltpu.SemaphoreType.DMA((3, acts[0].shape[0])),
            pltpu.VMEM((2, tokens, 1), f32),
        ],
        out_shape=[jax.ShapeDtypeStruct((1, number), f32)] * 2,
        compiler_params=pltpu.CompilerParams(vmem_limit_bytes=48 * 1024 * 1024),
        name="scores",
    )(chips_at, tiles_at, core, mine, more, *weights, *acts, eig, left, *rights)


def cut_kernel(*refs, cuts, count):
    sources, outs, sems = refs[:count], refs[count:-1], refs[-1]
    copies = [
        pltpu.make_async_copy(
            sources[source].at[pl.ds(start, size)], outs[out].at[pl.ds(to, size)], sems.at[at]
        )
        for at, (source, start, size, out, to) in enumerate(cuts)
    ]
    for copy in copies:
        copy.start()
    for copy in copies:
        copy.wait()


def cut_out(arrays, cuts):
    cols = arrays[0].shape[1]
    lengths = {}
    for _, _, size, out, to in cuts:
        lengths[out] = max(lengths.get(out, 0), to + size)
    return pl.pallas_call(
        functools.partial(cut_kernel, cuts=cuts, count=len(arrays)),
        in_specs=[pl.BlockSpec(memory_space=pltpu.HBM)] * len(arrays),
        out_specs=[pl.BlockSpec(memory_space=pltpu.VMEM)] * len(lengths),
        out_shape=[
            jax.ShapeDtypeStruct((lengths[out], cols), arrays[0].dtype)
            for out in range(len(lengths))
        ],
        scratch_shapes=[pltpu.SemaphoreType.DMA((len(cuts),))],
        name="cut",
    )(*arrays)


def accumulate_kernel(places_ref, mine, theirs, *refs, plan, count, carried):
    pieces = refs[:count]
    out_ref, grads_ref, basis_ref, sems = refs[count + carried : count + carried + 4]
    tokens = mine.shape[0]
    rows = sum(deep for _, deep, _, _ in plan[0])
    bounds = list(range(len(plan), 0, -2))[::-1]
    starts = [0] + bounds[:-1]

    groups = []
    used = 0
    for first, last in zip(starts, bounds):
        group = []
        for index in range(first, last):
            column = pl.multiple_of(places_ref[index] * rows, 128)
            for row, source in ((0, theirs), (tokens, mine)):
                group.append(
                    pltpu.make_async_copy(
                        source.at[:, pl.ds(column, rows)],
                        grads_ref.at[pl.ds(row, tokens), pl.ds(index * rows, rows)],
                        sems.at[used],
                    )
                )
                used += 1
            for offset, deep, piece, piece_row in plan[index]:
                group.append(
                    pltpu.make_async_copy(
                        pieces[piece].at[pl.ds(piece_row, deep)],
                        basis_ref.at[pl.ds(index * rows + offset, deep)],
                        sems.at[used],
                    )
                )
                used += 1
        groups.append(group)
    for group in groups:
        for copy in group:
            copy.start()
    if carried:
        before_ref = refs[-1]
        carry = pltpu.make_async_copy(refs[count], before_ref, sems.at[used])
        carry.start()
    total = None
    for first, last, group in zip(starts, bounds, groups):
        for copy in group:
            copy.wait()
        product = jnp.dot(
            grads_ref[:, first * rows : last * rows],
            basis_ref[first * rows : last * rows, :],
            preferred_element_type=f32,
        )
        total = product if total is None else total + product
    if carried:
        carry.wait()
        total = total + before_ref[...]
    out_ref[...] = total.astype(out_ref.dtype)


def accumulate(places, mine, theirs, plan, pieces, carried, kind, near=False):
    tokens = mine.shape[0]
    rows = sum(deep for _, deep, _, _ in plan[0])
    cols = pieces[0].shape[1]
    held = pl.BlockSpec(memory_space=pltpu.VMEM)
    anywhere = pl.BlockSpec(memory_space=pltpu.HBM)
    copies = sum(2 + len(cuts) for cuts in plan) + 1
    return pl.pallas_call(
        functools.partial(
            accumulate_kernel, plan=plan, count=len(pieces), carried=len(carried)
        ),
        in_specs=[
            pl.BlockSpec(memory_space=pltpu.SMEM),
            *[anywhere] * 2,
            *[held if near else anywhere] * len(pieces),
            *[anywhere] * len(carried),
        ],
        out_specs=held,
        out_shape=jax.ShapeDtypeStruct((2 * tokens, cols), kind),
        scratch_shapes=[
            pltpu.VMEM((2 * tokens, len(plan) * rows), bf16),
            pltpu.VMEM((len(plan) * rows, cols), bf16),
            pltpu.SemaphoreType.DMA((copies,)),
            *[pltpu.VMEM((2 * tokens, cols), f32) for _ in carried],
        ],
        compiler_params=pltpu.CompilerParams(vmem_limit_bytes=62 * 1024 * 1024),
        name="accumulate",
    )(places, mine, theirs, *pieces, *carried)


def per_device(
    doc_ids,
    doc_lengths,
    activations,
    out_grads,
    input_basis,
    output_basis,
    eigenvalues,
    query_left,
    query_right,
):
    tokens = activations.shape[0]
    rows, cols = output_basis.shape
    queries, rank, kin = query_left.shape
    n_y, n_zl = lax.axis_size("y"), lax.axis_size("zl")
    n_x = lax.axis_size("x")
    y, zl, core = lax.axis_index("y"), lax.axis_index("zl"), lax.axis_index("c")
    zh, x = lax.axis_index("zh"), lax.axis_index("x")
    chips = n_y * n_zl
    tile = 128

    def forth(v):
        return shifted(v, "y", 1)

    def back(v):
        return shifted(v, "y", -1)

    def across(v):
        return shifted(v, "zl", 1)

    def sibling(v):
        return shifted(v, "c", 1)

    def chip(dy, dz):
        return ((y + dy) % n_y) * n_zl + (zl + dz) % n_zl

    def places(*relative):
        return jnp.stack([2 * chip(dy, dz) + core for dy, dz in relative]).astype(jnp.int32)

    def x_shift(v, step):
        return shifted(v, "x", step)

    mine_left = lax.dynamic_index_in_dim(query_left, x, 0, keepdims=False)
    other_left = across(mine_left)
    left_pair = jnp.where(
        zl == 0, jnp.stack([mine_left, other_left]), jnp.stack([other_left, mine_left])
    )
    left_dp = lax.all_gather(left_pair, "y", axis=0)

    grads_peer = sibling(out_grads)
    share = lax.dot_general(
        input_basis, activations, (((0,), (1,)), ((), ())), preferred_element_type=f32
    ).astype(bf16)
    other = shifted(share, "zh", 1)

    block = jnp.concatenate([output_basis, query_right.reshape(queries * rank, cols)], axis=0)
    before, after = forth(block), back(block)
    half, most = 4 * tile, 5 * tile
    basis_z, right_z, other, left_pair = lax.optimization_barrier(
        (output_basis, query_right, other, left_pair)
    )
    beside_head = across(basis_z[:most])
    block_end = jnp.concatenate([basis_z[most:], right_z.reshape(queries * rank, cols)], axis=0)

    pair = jnp.where(zh == 0, jnp.stack([share, other]), jnp.stack([other, share]))
    weights = token_weights(doc_ids, doc_lengths)
    weights_peer = sibling(weights)
    pair, grads_peer, weights_peer = lax.optimization_barrier((pair, grads_peer, weights_peer))
    pair_before, pair_after = x_shift(pair, 1), x_shift(pair, -1)
    left_dp, pair_before, pair_after = lax.optimization_barrier((left_dp, pair_before, pair_after))
    left_chips = left_dp.reshape(chips, rank, kin)
    pair_far_0 = x_shift(pair_before[:1], 1)
    pair_far_1 = x_shift(pair_after[1:], -1)
    n_zh = lax.axis_size("zh")
    tiles_at = jnp.stack(
        [h * n_x + (x + dx) % n_x for dx in (0, -1, 1) for h in range(n_zh)]
        + [h * n_x + (x + 2) % n_x for h in range(n_zh)]
    ).astype(jnp.int32)
    chips_at = jnp.stack(
        [
            chip(0, 0), chip(3, 0), chip(1, 0), chip(0, 1),
            chip(3, 1), chip(1, 1), chip(2, 0), chip(2, 1),
        ]
    ).astype(jnp.int32)
    core_at = core.reshape(1).astype(jnp.int32)
    places_a = places((0, 0), (3, 0), (1, 0), (0, 1))
    places_c = places((2, 0), (3, 1), (1, 1))
    places_d = places((2, 1))
    weights = weights.reshape(tokens, 1)
    weights_peer = weights_peer.reshape(tokens, 1)
    (
        before, after, beside_head, block_end, weights, weights_peer, left_chips, pair_far_0,
        pair_far_1, tiles_at, chips_at, core_at, places_a, places_c, places_d,
    ) = lax.optimization_barrier(
        (
            before, after, beside_head, block_end, weights, weights_peer, left_chips, pair_far_0,
            pair_far_1, tiles_at, chips_at, core_at, places_a, places_c, places_d,
        )
    )

    left = lax.all_gather(left_chips, "x", axis=0)
    beside_end = across(block_end)
    before_beside_a = forth(beside_head)
    length = before.shape[0]
    end = length - most
    before_head, after_tail, both_ends = cut_out(
        (before, after),
        (
            (0, 0, half, 0, 0),
            (1, half, length - half, 1, 0),
            (0, most, end, 2, 0),
            (1, most, end, 2, end),
        ),
    )
    after_tail, beside_late = lax.optimization_barrier((after_tail, beside_head))
    far_a, far_b = forth(before_head), back(after_tail)
    after_beside_a = back(beside_late)
    beside_ends = across(both_ends)
    acts = jnp.concatenate([pair, pair_before, pair_after, pair_far_0, pair_far_1])
    acts = jnp.concatenate([pair, pair_before, pair_after, pair_far_0, pair_far_1])
    sums = accumulate(
        places_a, out_grads, grads_peer,
        (
            ((0, rows, 0, 0),),
            ((0, rows, 1, 0),),
            ((0, rows, 2, 0),),
            ((0, most, 3, 0), (most, rows - most, 4, 0)),
        ),
        (output_basis, before, after, beside_head, beside_end), (), f32,
    )
    far_b, sums, acts = lax.optimization_barrier((far_b, sums, acts))

    (part_a,) = cut_out((before_beside_a,), ((0, 0, 3 * tile, 0, 0),))
    (part_b,) = cut_out((after_beside_a,), ((0, 3 * tile, 2 * tile, 0, 0),))
    (part_c,) = cut_out((far_b,), ((0, most - half, end, 0, 0),))
    far_beside_a, far_beside_b, far_beside_c = forth(part_a), back(part_b), across(part_c)
    acts_peer = sibling(acts)
    sums = accumulate(
        places_c, out_grads, grads_peer,
        (
            ((0, half, 0, 0), (half, rows - half, 1, 0)),
            ((0, most, 2, 0), (most, rows - most, 4, 0)),
            ((0, most, 3, 0), (most, rows - most, 4, end)),
        ),
        (far_a, far_b, before_beside_a, after_beside_a, beside_ends), (sums,), f32,
    )

    mine = accumulate(
        places_d, out_grads, grads_peer,
        (((0, 3 * tile, 0, 0), (3 * tile, 2 * tile, 1, 0), (most, rows - most, 2, 0)),),
        (far_beside_a, far_beside_b, far_beside_c), (sums,), bf16, near=True,
    )
    more = sibling(mine)

    rights = (block, before, after, beside_end, beside_ends, far_b, far_beside_c)
    right_rows = (
        (0, rows), (1, rows), (2, rows), (3, end - tile), (4, end - tile), (4, 2 * end - tile),
        (5, far_b.shape[0] - tile), (6, end - tile),
    )
    values, values_peer = scores_of(
        chips_at, tiles_at, core_at, mine, more,
        (weights, weights_peer), (acts, acts_peer),
        eigenvalues, left, rights, right_rows, queries * 2 * chips,
    )
    values = values + sibling(values_peer)
    values = values + lax.ppermute(values, "x", [(i, i ^ 1) for i in range(n_x)])
    values = values + lax.ppermute(values, "x", [(i, n_x - 1 - i) for i in range(n_x)])
    return values + shifted(values, "zh", 1)


def solution(mesh):
    parts = Mesh(mesh.devices.reshape(4, 2, 2, 2, 4), ("y", "zl", "c", "zh", "x"))
    dp, mp = ("y", "zl", "c"), ("zh", "x")
    return jax.shard_map(
        per_device,
        mesh=parts,
        in_specs=(
            P(dp, None),
            P(dp),
            P(dp, None),
            P(dp, None),
            P(None, mp),
            P(dp, mp),
            P(None, mp),
            P(dp, None, None),
            P(dp, None, mp),
        ),
        out_specs=P(dp, None),
        check_vma=False,
    )
```

```python
import functools

import jax
import jax.numpy as jnp
from jax import lax
from jax.experimental import pallas as pl
from jax.experimental.pallas import tpu as pltpu
from jax.sharding import Mesh, PartitionSpec as P

damping = 0.5
f32 = jnp.float32
bf16 = jnp.bfloat16


def shifted(value, axis, step):
    size = lax.axis_size(axis)
    return lax.ppermute(value, axis, [(i, (i + step) % size) for i in range(size)])


def token_weights(doc_ids, doc_lengths):
    positions = jnp.arange(doc_ids.shape[1], dtype=jnp.int32)
    active = positions[None, :] < doc_lengths[:, None]
    matches = (doc_ids[:, :, None] == doc_ids[:, None, :]) & active[:, None, :]
    repeats = jnp.sum(matches.astype(f32), axis=2)
    return jnp.where(active, 1.0 / jnp.maximum(repeats, 1.0), 0.0)


def score_kernel(
    chips_ref, tiles_ref, core_ref, mine, more, own_weight, peer_weight, own_acts,
    peer_acts, eig, left, *refs, right_rows, count,
):
    rights = refs[:count]
    own_out, peer_out = refs[count : count + 2]
    (
        mine_ref, more_ref, acts_ref, eig_ref, left_ref, right_ref, scaled_ref, cond_ref, sums_ref,
        sems, tile_sems, weights_ref,
    ) = refs[count + 2 :]
    tiles, rows_in, tokens = own_acts.shape
    n_x, chips, rank, kin = left.shape
    cols = eig.shape[1]
    tile = 128
    queries = n_x * chips

    tile_copies = []
    for at in range(tiles):
        start = pl.multiple_of(tiles_ref[at] * rows_in, rows_in)
        tile_copies.append(
            [
                pltpu.make_async_copy(own_acts.at[at], acts_ref.at[0, at], tile_sems.at[0, at]),
                pltpu.make_async_copy(peer_acts.at[at], acts_ref.at[1, at], tile_sems.at[1, at]),
                pltpu.make_async_copy(
                    eig.at[pl.ds(start, rows_in), :],
                    eig_ref.at[pl.ds(start, rows_in), :],
                    tile_sems.at[2, at],
                ),
            ]
        )
    left_copy = pltpu.make_async_copy(left, left_ref, sems.at[3])
    right_copies = [
        [
            pltpu.make_async_copy(
                rights[piece].at[pl.ds(row + q * rank, rank), :],
                right_ref.at[q, chips_ref[index]],
                sems.at[4 + index * n_x + q],
            )
            for q in range(n_x)
        ]
        for index, (piece, row) in enumerate(right_rows)
    ]
    sum_copies = [
        pltpu.make_async_copy(mine, mine_ref, sems.at[4 + len(right_rows) * n_x]),
        pltpu.make_async_copy(more, more_ref, sems.at[5 + len(right_rows) * n_x]),
        pltpu.make_async_copy(own_weight, weights_ref.at[0], sems.at[0]),
        pltpu.make_async_copy(peer_weight, weights_ref.at[1], sems.at[1]),
    ]
    for copy in sum_copies:
        copy.start()
    for group in tile_copies:
        for copy in group:
            copy.start()
    left_copy.start()
    for group in right_copies:
        for copy in group:
            copy.start()

    for copy in sum_copies:
        copy.wait()
    for index, (mine_at, more_at) in enumerate(((tokens, 0), (0, tokens))):
        total = mine_ref[mine_at : mine_at + tokens, :].astype(f32)
        total = total + more_ref[more_at : more_at + tokens, :].astype(f32)
        rotated = total.astype(bf16).astype(f32)
        scaled_ref[index] = (weights_ref[index] * rotated).astype(bf16)

    for first in range(0, tiles, 2):
        pair = (first, first + 1)
        for at in pair:
            for copy in tile_copies[at]:
                copy.wait()
        starts = [pl.multiple_of(tiles_ref[at] * rows_in, rows_in) for at in pair]
        scales = [
            1.0 / (eig_ref[pl.ds(start, rows_in), :].astype(f32) + damping) for start in starts
        ]
        for index in range(2):
            acts = acts_ref[index, first : first + 2].reshape(2 * rows_in, tokens)
            gradient = jnp.dot(acts, scaled_ref[index], preferred_element_type=f32)
            for half_at, (start, scale) in enumerate(zip(starts, scales)):
                cond_ref[pl.ds(start, rows_in), index * cols : (index + 1) * cols] = (
                    gradient[half_at * rows_in : (half_at + 1) * rows_in] * scale
                ).astype(bf16)

    left_copy.wait()
    for group in right_copies:
        for copy in group:
            copy.wait()
    wide = 2 * tile
    half = n_x // 2
    for part in range(2):
        rows = left_ref[part * half : (part + 1) * half].reshape(half * chips * rank, kin)
        for at in range(0, 2 * cols, wide):
            mixture = jnp.dot(rows, cond_ref[:, at : at + wide], preferred_element_type=f32)
            for one in range(at, at + wide, tile):
                index, column = one // cols, one % cols
                right = right_ref[part * half : (part + 1) * half, :, :, column : column + tile]
                right = right.reshape(half * chips * rank, tile).astype(f32)
                product = mixture[:, one - at : one - at + tile] * right
                groups = jnp.sum(product.reshape(half * chips, rank, tile), axis=1)
                rows_at = part * half * chips
                if column == 0:
                    sums_ref[index, rows_at : rows_at + half * chips, :] = groups
                else:
                    sums_ref[index, rows_at : rows_at + half * chips, :] += groups

    number = own_out.shape[1]
    source = lax.broadcasted_iota(jnp.int32, (queries, number), 0)
    target = lax.broadcasted_iota(jnp.int32, (queries, number), 1)
    place = (2 * (source % chips) + core_ref[0]) * n_x + source // chips
    for index, out in enumerate((own_out, peer_out)):
        values = jnp.sum(sums_ref[index], axis=1, keepdims=True)
        out[...] = jnp.sum(jnp.where(place == target, values, 0.0), axis=0, keepdims=True)


def scores_of(
    chips_at, tiles_at, core, mine, more, weights, acts, eig, left, rights, right_rows, number
):
    tokens = acts[0].shape[2]
    kin, cols = eig.shape
    n_x, chips, rank, _ = left.shape
    scalars = pl.BlockSpec(memory_space=pltpu.SMEM)
    held = pl.BlockSpec(memory_space=pltpu.VMEM)
    anywhere = pl.BlockSpec(memory_space=pltpu.HBM)
    return pl.pallas_call(
        functools.partial(score_kernel, right_rows=right_rows, count=len(rights)),
        in_specs=[*[scalars] * 3, anywhere, held, *[anywhere] * (6 + len(rights))],
        out_specs=[held, held],
        scratch_shapes=[
            pltpu.VMEM(mine.shape, bf16),
            pltpu.VMEM(more.shape, bf16),
            pltpu.VMEM((2, *acts[0].shape), bf16),
            pltpu.VMEM(eig.shape, bf16),
            pltpu.VMEM(left.shape, bf16),
            pltpu.VMEM((n_x, chips, rank, cols), bf16),
            pltpu.VMEM((2, tokens, cols), bf16),
            pltpu.VMEM((kin, 2 * cols), bf16),
            pltpu.VMEM((2, n_x * chips, 128), f32),
            pltpu.SemaphoreType.DMA((6 + 8 * n_x,)),
            pltpu.SemaphoreType.DMA((3, acts[0].shape[0])),
            pltpu.VMEM((2, tokens, 1), f32),
        ],
        out_shape=[jax.ShapeDtypeStruct((1, number), f32)] * 2,
        compiler_params=pltpu.CompilerParams(vmem_limit_bytes=48 * 1024 * 1024),
        name="scores",
    )(chips_at, tiles_at, core, mine, more, *weights, *acts, eig, left, *rights)


def cut_kernel(*refs, cuts, count):
    sources, outs, sems = refs[:count], refs[count:-1], refs[-1]
    copies = [
        pltpu.make_async_copy(
            sources[source].at[pl.ds(start, size)], outs[out].at[pl.ds(to, size)], sems.at[at]
        )
        for at, (source, start, size, out, to) in enumerate(cuts)
    ]
    for copy in copies:
        copy.start()
    for copy in copies:
        copy.wait()


def cut_out(arrays, cuts):
    rest = arrays[0].shape[1:]
    lengths = {}
    for _, _, size, out, to in cuts:
        lengths[out] = max(lengths.get(out, 0), to + size)
    return pl.pallas_call(
        functools.partial(cut_kernel, cuts=cuts, count=len(arrays)),
        in_specs=[pl.BlockSpec(memory_space=pltpu.HBM)] * len(arrays),
        out_specs=[pl.BlockSpec(memory_space=pltpu.VMEM)] * len(lengths),
        out_shape=[
            jax.ShapeDtypeStruct((lengths[out], *rest), arrays[0].dtype)
            for out in range(len(lengths))
        ],
        scratch_shapes=[pltpu.SemaphoreType.DMA((len(cuts),))],
        name="cut",
    )(*arrays)


def accumulate_kernel(places_ref, mine, theirs, *refs, plan, rows, count, carried):
    pieces = refs[:count]
    out_ref, grads_ref, basis_ref, sems = refs[count + carried : count + carried + 4]
    tokens = mine.shape[0]

    groups = []
    bounds = [0]
    used = 0
    for chunks in plan:
        group = []
        at = bounds[-1]
        for block, offset, deep, piece, piece_row in chunks:
            column = pl.multiple_of(places_ref[block] * rows + offset, 128)
            for row, source in ((0, theirs), (tokens, mine)):
                group.append(
                    pltpu.make_async_copy(
                        source.at[:, pl.ds(column, deep)],
                        grads_ref.at[pl.ds(row, tokens), pl.ds(at, deep)],
                        sems.at[used],
                    )
                )
                used += 1
            group.append(
                pltpu.make_async_copy(
                    pieces[piece].at[pl.ds(piece_row, deep)],
                    basis_ref.at[pl.ds(at, deep)],
                    sems.at[used],
                )
            )
            used += 1
            at += deep
        groups.append(group)
        bounds.append(at)
    for group in groups:
        for copy in group:
            copy.start()
    if carried:
        before_ref = refs[-1]
        carry = pltpu.make_async_copy(refs[count], before_ref, sems.at[used])
        carry.start()
    total = None
    for first, last, group in zip(bounds, bounds[1:], groups):
        for copy in group:
            copy.wait()
        product = jnp.dot(
            grads_ref[:, first:last], basis_ref[first:last, :], preferred_element_type=f32
        )
        total = product if total is None else total + product
    if carried:
        carry.wait()
        total = total + before_ref[...]
    out_ref[...] = total.astype(out_ref.dtype)


def accumulate(places, mine, theirs, rows, plan, pieces, carried, kind, near=False):
    tokens = mine.shape[0]
    cols = pieces[0].shape[1]
    held = pl.BlockSpec(memory_space=pltpu.VMEM)
    anywhere = pl.BlockSpec(memory_space=pltpu.HBM)
    deep = sum(chunk[2] for chunks in plan for chunk in chunks)
    copies = 3 * sum(len(chunks) for chunks in plan) + 1
    return pl.pallas_call(
        functools.partial(
            accumulate_kernel, plan=plan, rows=rows, count=len(pieces), carried=len(carried)
        ),
        in_specs=[
            pl.BlockSpec(memory_space=pltpu.SMEM),
            *[anywhere] * 2,
            *[held if near else anywhere] * len(pieces),
            *[anywhere] * len(carried),
        ],
        out_specs=held,
        out_shape=jax.ShapeDtypeStruct((2 * tokens, cols), kind),
        scratch_shapes=[
            pltpu.VMEM((2 * tokens, deep), bf16),
            pltpu.VMEM((deep, cols), bf16),
            pltpu.SemaphoreType.DMA((copies,)),
            *[pltpu.VMEM((2 * tokens, cols), f32) for _ in carried],
        ],
        compiler_params=pltpu.CompilerParams(vmem_limit_bytes=62 * 1024 * 1024),
        name="accumulate",
    )(places, mine, theirs, *pieces, *carried)


def per_device(
    doc_ids,
    doc_lengths,
    activations,
    out_grads,
    input_basis,
    output_basis,
    eigenvalues,
    query_left,
    query_right,
):
    tokens = activations.shape[0]
    rows, cols = output_basis.shape
    queries, rank, kin = query_left.shape
    n_y, n_zl = lax.axis_size("y"), lax.axis_size("zl")
    n_x = lax.axis_size("x")
    y, zl, core = lax.axis_index("y"), lax.axis_index("zl"), lax.axis_index("c")
    zh, x = lax.axis_index("zh"), lax.axis_index("x")
    chips = n_y * n_zl
    tile = 128

    def forth(v):
        return shifted(v, "y", 1)

    def back(v):
        return shifted(v, "y", -1)

    def across(v):
        return shifted(v, "zl", 1)

    def sibling(v):
        return shifted(v, "c", 1)

    def chip(dy, dz):
        return ((y + dy) % n_y) * n_zl + (zl + dz) % n_zl

    def places(*relative):
        return jnp.stack([2 * chip(dy, dz) + core for dy, dz in relative]).astype(jnp.int32)

    def x_shift(v, step):
        return shifted(v, "x", step)

    mine_left = lax.dynamic_index_in_dim(query_left, x, 0, keepdims=False)
    other_left = across(mine_left)
    left_pair = jnp.where(
        zl == 0, jnp.stack([mine_left, other_left]), jnp.stack([other_left, mine_left])
    )
    left_dp = lax.all_gather(left_pair, "y", axis=0)

    grads_peer = sibling(out_grads)
    share = lax.dot_general(
        input_basis, activations, (((0,), (1,)), ((), ())), preferred_element_type=f32
    ).astype(bf16)
    other = shifted(share, "zh", 1)

    block = jnp.concatenate([output_basis, query_right.reshape(queries * rank, cols)], axis=0)
    before, after = forth(block), back(block)
    half, most = 4 * tile, 5 * tile
    basis_z, right_z, other, left_pair = lax.optimization_barrier(
        (output_basis, query_right, other, left_pair)
    )
    beside_head = across(basis_z[:most])
    block_end = jnp.concatenate([basis_z[most:], right_z.reshape(queries * rank, cols)], axis=0)

    pair = jnp.where(zh == 0, jnp.stack([share, other]), jnp.stack([other, share]))
    weights = token_weights(doc_ids, doc_lengths)
    weights_peer = sibling(weights)
    pair, grads_peer, weights_peer = lax.optimization_barrier((pair, grads_peer, weights_peer))
    pair_before, pair_after = x_shift(pair, 1), x_shift(pair, -1)
    left_dp, pair_before, pair_after = lax.optimization_barrier((left_dp, pair_before, pair_after))
    left_chips = left_dp.reshape(chips, rank, kin)
    pair_far_0 = x_shift(pair_before[:1], 1)
    pair_far_1 = x_shift(pair_after[1:], -1)
    n_zh = lax.axis_size("zh")
    tiles_at = jnp.stack(
        [h * n_x + (x + dx) % n_x for dx in (0, -1, 1) for h in range(n_zh)]
        + [h * n_x + (x + 2) % n_x for h in range(n_zh)]
    ).astype(jnp.int32)
    chips_at = jnp.stack(
        [
            chip(0, 0), chip(3, 0), chip(1, 0), chip(0, 1),
            chip(3, 1), chip(1, 1), chip(2, 0), chip(2, 1),
        ]
    ).astype(jnp.int32)
    core_at = core.reshape(1).astype(jnp.int32)
    places_a = places((0, 0), (3, 0), (1, 0), (0, 1))
    places_c = places((2, 0), (3, 1), (1, 1))
    places_d = places((2, 1))
    weights = weights.reshape(tokens, 1)
    weights_peer = weights_peer.reshape(tokens, 1)
    (
        before, after, beside_head, block_end, weights, weights_peer, left_chips, pair_far_0,
        pair_far_1, tiles_at, chips_at, core_at, places_a, places_c, places_d,
    ) = lax.optimization_barrier(
        (
            before, after, beside_head, block_end, weights, weights_peer, left_chips, pair_far_0,
            pair_far_1, tiles_at, chips_at, core_at, places_a, places_c, places_d,
        )
    )

    left = lax.all_gather(left_chips, "x", axis=0)
    beside_end = across(block_end)
    before_beside_a = forth(beside_head)
    length = before.shape[0]
    end = length - most
    (after_tail,) = cut_out((after,), ((0, half, length - half, 0, 0),))
    after_tail, beside_late, before, after = lax.optimization_barrier(
        (after_tail, beside_head, before, after)
    )
    before_head, both_ends = cut_out(
        (before, after), ((0, 0, half, 0, 0), (0, most, end, 1, 0), (1, most, end, 1, end))
    )
    far_a, far_b = forth(before_head), back(after_tail)
    after_beside_a = back(beside_late)
    beside_ends = across(both_ends)
    (acts,) = cut_out(
        (pair, pair_before, pair_after, pair_far_0, pair_far_1),
        ((0, 0, 2, 0, 0), (1, 0, 2, 0, 2), (2, 0, 2, 0, 4), (3, 0, 1, 0, 6), (4, 0, 1, 0, 7)),
    )
    (acts,) = cut_out(
        (pair, pair_before, pair_after, pair_far_0, pair_far_1),
        ((0, 0, 2, 0, 0), (1, 0, 2, 0, 2), (2, 0, 2, 0, 4), (3, 0, 1, 0, 6), (4, 0, 1, 0, 7)),
    )
    sums = accumulate(
        places_a, out_grads, grads_peer, rows,
        (
            ((0, 0, rows, 0, 0), (1, 0, rows, 1, 0)),
            ((2, 0, rows, 2, 0), (3, 0, most, 3, 0), (3, most, rows - most, 4, 0)),
        ),
        (output_basis, before, after, beside_head, beside_end), (), f32,
    )
    sums = accumulate(
        places_c, out_grads, grads_peer, rows,
        (((0, half, rows - half, 0, 0), (1, 0, most, 1, 0)),),
        (far_b, before_beside_a), (sums,), f32,
    )
    far_b, sums, acts = lax.optimization_barrier((far_b, sums, acts))

    (part_a,) = cut_out((before_beside_a,), ((0, 0, 3 * tile, 0, 0),))
    (part_b,) = cut_out((after_beside_a,), ((0, 3 * tile, 2 * tile, 0, 0),))
    (part_c,) = cut_out((far_b,), ((0, most - half, end, 0, 0),))
    far_beside_a, far_beside_b, far_beside_c = forth(part_a), back(part_b), across(part_c)
    acts_peer = sibling(acts)
    sums = accumulate(
        places_c, out_grads, grads_peer, rows,
        (
            ((0, 0, half, 0, 0),),
            (
                (1, most, rows - most, 2, 0),
                (2, 0, most, 1, 0),
                (2, most, rows - most, 2, end),
            ),
        ),
        (far_a, after_beside_a, beside_ends), (sums,), f32,
    )

    mine = accumulate(
        places_d, out_grads, grads_peer, rows,
        (
            (
                (0, 0, 3 * tile, 0, 0),
                (0, 3 * tile, 2 * tile, 1, 0),
                (0, most, rows - most, 2, 0),
            ),
        ),
        (far_beside_a, far_beside_b, far_beside_c), (sums,), bf16, near=True,
    )
    more = sibling(mine)

    rights = (block, before, after, beside_end, beside_ends, far_b, far_beside_c)
    right_rows = (
        (0, rows), (1, rows), (2, rows), (3, end - tile), (4, end - tile), (4, 2 * end - tile),
        (5, far_b.shape[0] - tile), (6, end - tile),
    )
    values, values_peer = scores_of(
        chips_at, tiles_at, core_at, mine, more,
        (weights, weights_peer), (acts, acts_peer),
        eigenvalues, left, rights, right_rows, queries * 2 * chips,
    )
    values = values + sibling(values_peer)
    values = values + lax.ppermute(values, "x", [(i, i ^ 1) for i in range(n_x)])
    values = values + lax.ppermute(values, "x", [(i, n_x - 1 - i) for i in range(n_x)])
    return values + shifted(values, "zh", 1)


def solution(mesh):
    parts = Mesh(mesh.devices.reshape(4, 2, 2, 2, 4), ("y", "zl", "c", "zh", "x"))
    dp, mp = ("y", "zl", "c"), ("zh", "x")
    return jax.shard_map(
        per_device,
        mesh=parts,
        in_specs=(
            P(dp, None),
            P(dp),
            P(dp, None),
            P(dp, None),
            P(None, mp),
            P(dp, mp),
            P(None, mp),
            P(dp, None, None),
            P(dp, None, mp),
        ),
        out_specs=P(dp, None),
        check_vma=False,
    )
```
